32 devices in a mesh: rows: 16 (over z, y, x), layer: 2 (over core).
Axes of the slice: x: 2, y: 2, z: 4, core: 2. Of those that a mesh axis runs over, the one named last changes fastest.
Arguments:
- density: bfloat16 [256, 33, 64, 64], P('rows'), as said below
- col_index: int32 [256, 33], replicated, may hold values from 0 to 255, as said below
- counts: int32 [256], replicated, may hold values from 1 to 33, as said below
- domain: int32 [256], replicated, may hold values from 0 to 63
Outputs:
- square: bfloat16 [256, 33, 64, 64], P(('rows', 'layer'))
- populations: float32 [64, 64], P(('rows', 'layer'))
- traces: float32 [2], replicated
The draws below stay inside these ranges and needn't reach their ends.
Inputs may be any that keep to these rules, and one draw needn't show every extreme that they name: `col_index`: the pattern is symmetric, holds every diagonal block, and every stored column lies within 16 block rows of its row, counted cyclically over 256. The first counts[i] slots of row i hold distinct columns in rising order of their cyclic distance from -16 to 16; the other slots hold further distinct columns within that reach. `counts`: some row holds all 33 slots. `density`: block X[j, i] is the transpose of X[i, j]; slots that are not live hold zeros.
All inputs are finite; a program needn't handle non-finite values.
Results may differ from the reference program's by a relative error of at most 0.0018.
Values may be sent and summed in bfloat16 or wider, within the bound.
No kernel may reach another device: no remote copies, remote signals or barrier semaphores. Data moves between devices by JAX's collectives and lax.ppermute only.
A program may use at most 192 MiB of HBM per device.

```python
import jax
import jax.numpy as jnp
from jax import lax

B = 64
HB = 16
NNZ = 33
NB = 256
NDOM = 64


def pattern(key):
    seed_key = jax.random.fold_in(key, 11)
    key_region, key_links, key_center = jax.random.split(seed_key, 3)
    row_ids = jnp.arange(NB, dtype=jnp.int32)
    region = jax.random.randint(key_region, (NB // HB + 1,), 20, 95)
    levels = region[row_ids // HB]
    linked = jax.random.randint(key_links, (NB, HB), 0, 100) < levels[:, None]
    center = jax.random.randint(key_center, (), 0, NB)
    offsets = jnp.arange(1, HB + 1, dtype=jnp.int32)
    upper_rows = (row_ids[:, None] + offsets[None, :]) % NB
    linked = linked | (row_ids[:, None] == center) | (upper_rows == center)
    reversed_offsets = offsets[::-1]
    below = linked[(row_ids[:, None] - reversed_offsets[None, :]) % NB, reversed_offsets - 1]
    present = jnp.concatenate([below, jnp.ones((NB, 1), dtype=bool), linked], axis=1)
    candidate = jnp.concatenate([-reversed_offsets, jnp.zeros((1,), jnp.int32), offsets])
    ranking = jnp.argsort(1 - present.astype(jnp.int32), axis=1, stable=True)
    shifted = jnp.take_along_axis(jnp.broadcast_to(candidate[None, :], (NB, NNZ)), ranking, axis=1)
    columns = ((row_ids[:, None] + shifted) % NB).astype(jnp.int32)
    totals = jnp.sum(present.astype(jnp.int32), axis=1).astype(jnp.int32)
    return (columns, totals)


def draw_col_index(key, part):
    return pattern(key)[0]


def draw_counts(key, part):
    return pattern(key)[1]


def draw_density(key, part):
    columns, totals = pattern(key)
    row_ids = jnp.arange(NB, dtype=jnp.int32)[:, None]
    lower_row = jnp.minimum(row_ids, columns)
    upper_row = jnp.maximum(row_ids, columns)
    pair_id = (lower_row * NB + upper_row).reshape(-1)
    pair_key = jax.random.fold_in(key, 23)

    def draw_block(pair):
        block_key = jax.random.fold_in(pair_key, pair)
        return jax.random.normal(block_key, (B, B), jnp.float32)
    noise = jax.vmap(draw_block)(pair_id).reshape(NB, NNZ, B, B)
    flipped = jnp.swapaxes(noise, -1, -2)
    noise = jnp.where((row_ids > columns)[:, :, None, None], flipped, noise)
    on_diag = (row_ids == columns)[:, :, None, None]
    symmetric = (noise + flipped) * 0.7071
    blocks = jnp.where(on_diag, symmetric, noise) * (0.5 / B ** 0.5)
    rise = 0.5 + jnp.arange(NB, dtype=jnp.float32) / NB
    occupation = jax.random.uniform(jax.random.fold_in(key, 29), (NB, B), jnp.float32, 0.05, 0.95)
    occupation = occupation * rise[:, None]
    unit_diag = jnp.eye(B, dtype=jnp.float32)
    blocks = blocks + jnp.where(on_diag, occupation[:, None, :, None] * unit_diag[None, None, :, :], 0.0)
    live_slot = jnp.arange(NNZ)[None, :] < totals[:, None]
    blocks = jnp.where(live_slot[:, :, None, None], blocks, 0.0)
    return blocks.astype(jnp.bfloat16)


def with_ends(drawn, stream_key, smallest, largest):
    index_at = [jax.random.randint(jax.random.fold_in(stream_key, axis), (), 0, length) for axis, length in enumerate(drawn.shape)]
    main_axis = drawn.shape.index(max(drawn.shape))
    beside = index_at[:main_axis] + [(index_at[main_axis] + 1) % drawn.shape[main_axis]] + index_at[main_axis + 1:]
    return drawn.at[tuple(index_at)].set(smallest).at[tuple(beside)].set(largest)


def setup_inputs(seed: int = 0) -> dict:
    key_of = jax.random.split(jax.random.key(seed), 5)
    density = draw_density(jax.random.fold_in(key_of[4], 71), 0)
    col_index = draw_col_index(jax.random.fold_in(key_of[4], 71), 0)
    counts = draw_counts(jax.random.fold_in(key_of[4], 71), 0)
    domain = with_ends(jax.random.randint(key_of[3], (NB,), 0, NDOM), jax.random.fold_in(key_of[3], 1), 0, NDOM - 1).astype(jnp.int32)
    return dict(density=density, col_index=col_index, counts=counts, domain=domain)


def reference(density, col_index, counts, domain):
    slot_range = jnp.arange(NNZ, dtype=jnp.int32)

    def row_product(row_id):
        row_cols = col_index[row_id]
        row_count = counts[row_id]
        partner_rows = density[row_cols]
        partner_cols = col_index[row_cols]
        partner_count = counts[row_cols]
        select = (partner_cols[:, None, :] == row_cols[None, :, None])
        select = select & (slot_range[None, None, :] < partner_count[:, None, None])
        select = select & (slot_range[:, None, None] < row_count) & (slot_range[None, :, None] < row_count)
        picked = jnp.einsum("amb,abxy->amxy", select.astype(jnp.float32), partner_rows.astype(jnp.float32)).astype(jnp.bfloat16)
        product = jnp.einsum("apx,amxy->mpy", density[row_id].astype(jnp.float32), picked.astype(jnp.float32))
        return product.astype(jnp.bfloat16)

    square = lax.map(row_product, jnp.arange(NB, dtype=jnp.int32))
    diag_mask = (col_index == jnp.arange(NB, dtype=jnp.int32)[:, None]) & (slot_range[None, :] < counts[:, None])
    diag_mask = diag_mask.astype(jnp.float32)[:, :, None]
    diag_square = jnp.sum(diag_mask * jnp.diagonal(square, axis1=2, axis2=3).astype(jnp.float32), axis=1)
    diag_density = jnp.sum(diag_mask * jnp.diagonal(density, axis1=2, axis2=3).astype(jnp.float32), axis=1)
    populations = jax.ops.segment_sum(diag_square, domain, NDOM)
    traces = jnp.stack([jnp.sum(diag_density), jnp.sum(diag_square)]) / (NB * B)
    return square, populations, traces
```

```python
import functools

import jax
import jax.numpy as jnp
from jax import lax
from jax.experimental import pallas as pl
from jax.experimental.pallas import tpu as pltpu
from jax.sharding import PartitionSpec as P

DOM_DEV = 2
AXES = ("rows", "layer")
SYM = [(u, t) for u in range(4) for t in range(u, 4)]
FULL = [(u, t) for u in range(4) for t in range(4)]
NT = (((1,), (1,)), ((), ()))
BF = jnp.bfloat16
F32 = jnp.float32
IN_HBM = pl.BlockSpec(memory_space=pltpu.HBM)


def pack_kernel(groups, meta, density, *rest):
    outs, buf, sems = rest[-2 - len(groups) : -2], rest[-2], rest[-1]
    layer = lax.axis_index("layer")
    starts = (8 * layer, 8 * (1 - layer))
    base = 0
    for g, (tiles, near, far) in enumerate(groups):
        row, col = starts[near], starts[far]
        for n, (u, t) in enumerate(tiles):
            for r in range(2):
                for s in range(2):
                    k = row + 2 * u + r
                    slot = meta[k, (col - row) + 2 * t + s - 2 * u - r + 16]
                    at = base + 4 * n + 2 * r + s
                    pltpu.make_async_copy(density.at[k, slot], buf.at[at], sems.at[g]).start()
        base += 4 * len(tiles)
    base = 0
    for g, (tiles, _, _) in enumerate(groups):
        span = buf.at[pl.ds(base, 4 * len(tiles))]
        pltpu.make_async_copy(span, span, sems.at[g]).wait()
        for n in range(len(tiles)):
            for r in range(2):
                at = base + 4 * n + 2 * r
                outs[g][n, 64 * r : 64 * r + 64, :] = jnp.concatenate(
                    [buf[at], buf[at + 1]], axis=1
                )
        base += 4 * len(tiles)


def pack(groups, meta, density, *after):
    sizes = [len(tiles) for tiles, _, _ in groups]
    return pl.pallas_call(
        functools.partial(pack_kernel, groups),
        grid_spec=pltpu.PrefetchScalarGridSpec(
            num_scalar_prefetch=1,
            grid=(1,),
            in_specs=[IN_HBM] * (1 + len(after)),
            out_specs=[pl.BlockSpec((n, 128, 128), lambda i, m: (0, 0, 0)) for n in sizes],
            scratch_shapes=[
                pltpu.VMEM((4 * sum(sizes), 64, 64), BF),
                pltpu.SemaphoreType.DMA((len(sizes),)),
            ],
        ),
        out_shape=[jax.ShapeDtypeStruct((n, 128, 128), BF) for n in sizes],
        compiler_params=pltpu.CompilerParams(vmem_limit_bytes=58 << 20),
        cost_estimate=pl.CostEstimate(
            flops=0, bytes_accessed=sum(sizes) << 17, transcendentals=0
        ),
        name="pack",
    )(meta, density, *after)


def spread(slots, block, own, first, at, k):
    zero = jnp.zeros((64, 64), BF)
    for r in range(2):
        rows = pl.ds(pl.multiple_of(at + 64 * r, 64), 64)
        total = jnp.zeros((64, 128), F32)
        for pp in range(17):
            halves = []
            for s in range(2):
                d = 2 * pp + s - r
                halves.append(block(r, slots[k + r, d]) if 0 <= d <= 32 else zero)
            pair = jnp.concatenate(halves, axis=1)
            own[first + pp, rows, :] = pair
            wide_pair = pair.astype(F32)
            total += wide_pair * wide_pair
        yield r, total


def diag_kernel(meta, domain, rows_ref, _, out_ref, own, sums):
    step = pl.program_id(0)
    layer = lax.axis_index("layer")
    start = 16 * lax.axis_index("rows")
    k = 8 * layer + 2 * step

    @pl.when(step == 0)
    def _():
        out_ref[...] = jnp.zeros_like(out_ref)
        sums[...] = jnp.zeros_like(sums)

        @pl.loop(0, 24)
        def _(p):
            own[p] = jnp.zeros(own.shape[1:], BF)

    eye = lax.broadcasted_iota(jnp.int32, (64, 64), 0) == lax.broadcasted_iota(
        jnp.int32, (64, 64), 1
    )
    sub = lax.broadcasted_iota(jnp.int32, (8, 64), 0)

    def block(r, slot):
        return rows_ref[r, slot]

    for r, total in spread(meta, block, own, 4 * layer + step, 128 * step, k):
        column = jnp.sum(total, axis=1, keepdims=True)
        squares = jnp.sum(jnp.where(eye, column, 0.0), axis=0, keepdims=True)
        squares = squares.astype(BF).astype(F32)
        middle = block(r, meta[k + r, 16]).astype(F32)
        diagonal = jnp.sum(jnp.where(eye, middle, 0.0), axis=0, keepdims=True)
        target = domain[start + k + r]
        owner = target // DOM_DEV
        place = target - owner * DOM_DEV
        out_ref[owner, :, 0:64] = out_ref[owner, :, 0:64] + jnp.where(sub == place, squares, 0.0)
        sums[:, 0:64] = sums[:, 0:64] + jnp.where(
            sub == DOM_DEV, diagonal, jnp.where(sub == DOM_DEV + 1, squares, 0.0)
        )

    @pl.when(step == pl.num_programs(0) - 1)
    def _():
        out_ref[...] = out_ref[...] + sums[...][None]


def diagonals(meta, domain, density, after, devices):
    capacity = density.shape[1]
    return pl.pallas_call(
        diag_kernel,
        grid_spec=pltpu.PrefetchScalarGridSpec(
            num_scalar_prefetch=2,
            grid=(4,),
            in_specs=[
                pl.BlockSpec(
                    (2, capacity, 64, 64),
                    lambda i, m, d: (4 * lax.axis_index("layer") + i, 0, 0, 0),
                ),
                IN_HBM,
            ],
            out_specs=[
                pl.BlockSpec((devices, 8, 128), lambda i, m, d: (0, 0, 0)),
                pl.BlockSpec((24, 512, 128), lambda i, m, d: (0, 0, 0)),
            ],
            scratch_shapes=[pltpu.VMEM((8, 128), F32)],
        ),
        out_shape=[
            jax.ShapeDtypeStruct((devices, 8, 128), F32),
            jax.ShapeDtypeStruct((24, 512, 128), BF),
        ],
        compiler_params=pltpu.CompilerParams(vmem_limit_bytes=54 << 20),
        cost_estimate=pl.CostEstimate(flops=0, bytes_accessed=8 << 20, transcendentals=0),
        name="diagonals",
    )(meta, domain, density, after)


def octant(layer, q):
    return jnp.where(layer == 0, q, 5 - q)


def wide(ref, pair, rows):
    return jnp.concatenate([ref[pair, rows, :], ref[pair + 1, rows, :]], axis=1)


def local_kernel(meta, density, mine, _, part_ref, near_ref, rows_ref, sems, other):
    layer = lax.axis_index("layer")
    sib = 8 * (1 - layer)
    for k in range(8):
        pltpu.make_async_copy(density.at[sib + k], rows_ref.at[k], sems.at[k]).start()

    @pl.loop(0, 24)
    def _(p):
        other[p] = jnp.zeros(other.shape[1:], BF)

    @pl.loop(0, 4)
    def _(u):
        for r in range(2):
            k = 2 * u + r
            pltpu.make_async_copy(density.at[sib + k], rows_ref.at[k], sems.at[k]).wait()

        def block(r, slot):
            return rows_ref[2 * u + r, slot]

        for _ in spread(meta, block, other, 4 * (1 - layer) + u, 128 * u, sib + 2 * u):
            pass

    at = [4 * octant(layer, q) for q in range(5)]
    every = pl.ds(0, 512)

    def put(ref, base, half, value):
        ref[base + 2 * half] = value[:, 0:128].astype(ref.dtype)
        ref[base + 2 * half + 1] = value[:, 128:256].astype(ref.dtype)

    def left(ref, octs, rows):
        return jnp.concatenate([wide(ref, at[q] + 2 * h, rows) for q in octs for h in range(2)], axis=1)

    for base, octs, source in ((0, (0, 1, 2, 3, 4), mine), (4, (1, 2, 3, 4), other)):
        for half in range(2):
            right = left(source, octs, pl.ds(256 * half, 256))
            value = lax.dot_general(left(mine, octs, every), right, NT, preferred_element_type=F32)
            put(near_ref, base, half, value)

    sources = {2: mine, 3: other}
    for base, q, octs in ((0, 0, (2,)), (4, 1, (2, 3)), (8, 4, (2, 3))):
        for half in range(2):
            right = jnp.concatenate(
                [wide(sources[o], at[q] + 2 * half, every) for o in octs], axis=0
            )
            value = jnp.dot(left(mine, octs, every), right, preferred_element_type=F32)
            put(part_ref, base, half, value)


def local(meta, density, mine, after):
    capacity = density.shape[1]
    return pl.pallas_call(
        local_kernel,
        grid_spec=pltpu.PrefetchScalarGridSpec(
            num_scalar_prefetch=1,
            grid=(1,),
            in_specs=[IN_HBM, pl.BlockSpec((24, 512, 128), lambda i, m: (0, 0, 0)), IN_HBM],
            out_specs=[pl.BlockSpec((n, 512, 128), lambda i, m: (0, 0, 0)) for n in (12, 8)],
            scratch_shapes=[
                pltpu.VMEM((8, capacity, 64, 64), BF),
                pltpu.SemaphoreType.DMA((8,)),
                pltpu.VMEM((24, 512, 128), BF),
            ],
        ),
        out_shape=[
            jax.ShapeDtypeStruct((12, 512, 128), F32),
            jax.ShapeDtypeStruct((8, 512, 128), BF),
        ],
        compiler_params=pltpu.CompilerParams(vmem_limit_bytes=54 << 20),
        cost_estimate=pl.CostEstimate(
            flops=4 << 30, bytes_accessed=16 << 20, transcendentals=0
        ),
        name="local",
    )(meta, density, mine, after)


def unfold(tiles_ref, full_ref):
    for n, (u, t) in enumerate(SYM):
        tile = tiles_ref[n]
        full_ref[t, 128 * u : 128 * u + 128, :] = tile
        if t > u:
            full_ref[u, 128 * t : 128 * t + 128, :] = tile.T


def sides(left, starts):
    every = pl.ds(0, 512)
    return jnp.concatenate([wide(left, p + 2 * h, every) for p in starts for h in range(2)], axis=1)


def most_kernel(meta, counts, left, part, near, ss, ms, corner, out_ref, first_ref, y, full):
    layer = lax.axis_index("layer")
    start = 16 * lax.axis_index("rows")
    at = [4 * octant(layer, q) for q in range(5)]
    step = pl.program_id(0)

    @pl.when(step == 0)
    def _():
        for q in range(2):
            for p in range(4):
                y[at[2 + q] + p] = near[4 * q + p]
        every = pl.ds(0, 512)

        def put(q, base, half, value):
            for s in range(2):
                p = 2 * half + s
                total = part[base + p] + value[:, 128 * s : 128 * s + 128]
                if q == 0:
                    first_ref[p] = total
                else:
                    y[at[q] + p] = total.astype(BF)

        unfold(corner, full)
        for half in range(2):
            right = wide(full, 2 * half, every)
            put(4, 8, half, jnp.dot(sides(left, at[4:5]), right, preferred_element_type=F32))
        unfold(ss, full)
        for half in range(2):
            top = jnp.concatenate(
                [
                    jnp.concatenate([ms[4 * u + 2 * half], ms[4 * u + 2 * half + 1]], axis=1)
                    for u in range(4)
                ],
                axis=0,
            )
            right = jnp.concatenate([top, wide(full, 2 * half, every)], axis=0)
            put(1, 4, half, jnp.dot(sides(left, at[0:2]), right, preferred_element_type=F32))
        for half in range(2):
            right = jnp.concatenate(
                [
                    jnp.concatenate([ms[4 * u + t] for t in range(4)], axis=1)
                    for u in (2 * half, 2 * half + 1)
                ],
                axis=0,
            )
            value = lax.dot_general(sides(left, at[1:2]), right, NT, preferred_element_type=F32)
            put(0, 0, half, value)

    for r in range(2):
        i = 2 * step + r
        k = 8 * layer + i
        count = counts[start + k]
        rows = pl.ds(pl.multiple_of(64 * i, 64), 64)
        for d in range(33):
            pair = 4 * layer + step + (r + d) // 2
            odd = (r + d) % 2
            slot = meta[k, d]
            block = y[pair, rows, :][:, 64 * odd : 64 * odd + 64]
            out_ref[r, slot] = jnp.where(slot < count, block, jnp.zeros_like(block))


def most(meta, counts, parts, tiles, capacity):
    def whole(n, rows):
        return pl.BlockSpec((n, rows, 128), lambda i, m, c: (0, 0, 0))

    return pl.pallas_call(
        most_kernel,
        grid_spec=pltpu.PrefetchScalarGridSpec(
            num_scalar_prefetch=2,
            grid=(4,),
            in_specs=[whole(24, 512), whole(12, 512), whole(8, 512)]
            + [whole(n, 128) for n in (10, 16, 10)],
            out_specs=[
                pl.BlockSpec((2, capacity, 64, 64), lambda i, m, c: (i, 0, 0, 0)),
                whole(4, 512),
            ],
            scratch_shapes=[
                pltpu.VMEM((24, 512, 128), BF),
                pltpu.VMEM((4, 512, 128), BF),
            ],
        ),
        out_shape=[
            jax.ShapeDtypeStruct((8, capacity, 64, 64), BF),
            jax.ShapeDtypeStruct((4, 512, 128), F32),
        ],
        compiler_params=pltpu.CompilerParams(vmem_limit_bytes=40 << 20),
        cost_estimate=pl.CostEstimate(
            flops=1 << 30, bytes_accessed=12 << 20, transcendentals=0
        ),
        name="most",
    )(meta, counts, *parts, *tiles)


def last_kernel(meta, counts, first, left, mm, _, out_ref, full, y, stage, sem):
    layer = lax.axis_index("layer")
    start = 16 * lax.axis_index("rows")
    unfold(mm, full)
    for half in range(2):
        right = wide(full, 2 * half, pl.ds(0, 512))
        value = jnp.dot(sides(left, (4 * octant(layer, 0),)), right, preferred_element_type=F32)
        for s in range(2):
            p = 2 * half + s
            y[p] = (first[p] + value[:, 128 * s : 128 * s + 128]).astype(BF)
    sign = 1 - 2 * layer
    base = jnp.where(layer == 0, 0, 32)
    for i in range(8):
        k = 8 * layer + i
        count = counts[start + k]
        for e in range(8):
            at = 8 * i + e

            @pl.when((e - i) * sign >= 0)
            def _():
                slot = meta[k, base + e - i]
                block = y[e // 2, 64 * i : 64 * i + 64, :][:, 64 * (e % 2) : 64 * (e % 2) + 64]
                stage[at] = jnp.where(slot < count, block, jnp.zeros_like(block))
                pltpu.make_async_copy(stage.at[at], out_ref.at[i, slot], sem).start()

    done = stage.at[pl.ds(0, 36)]
    pltpu.make_async_copy(done, done, sem).wait()


def last(meta, counts, first, left, mm, square):
    def whole(n, rows):
        return pl.BlockSpec((n, rows, 128), lambda i, m, c: (0, 0, 0))

    return pl.pallas_call(
        last_kernel,
        grid_spec=pltpu.PrefetchScalarGridSpec(
            num_scalar_prefetch=2,
            grid=(1,),
            in_specs=[whole(4, 512), whole(24, 512), whole(10, 128), IN_HBM],
            out_specs=IN_HBM,
            scratch_shapes=[
                pltpu.VMEM((4, 512, 128), BF),
                pltpu.VMEM((4, 512, 128), BF),
                pltpu.VMEM((64, 64, 64), BF),
                pltpu.SemaphoreType.DMA,
            ],
        ),
        out_shape=jax.ShapeDtypeStruct(square.shape, BF),
        input_output_aliases={5: 0},
        compiler_params=pltpu.CompilerParams(vmem_limit_bytes=16 << 20),
        cost_estimate=pl.CostEstimate(
            flops=1 << 28, bytes_accessed=3 << 20, transcendentals=0
        ),
        name="last",
    )(meta, counts, first, left, mm, square)


def totals_kernel(scale, sent, populations_ref, traces_ref):
    total = jnp.sum(sent[...], axis=0)[:, 0:64]
    populations_ref[...] = total[0:DOM_DEV]
    for n in range(2):
        traces_ref[n] = jnp.sum(total[DOM_DEV + n : DOM_DEV + n + 1]) * scale


def totals(gathered, scale):
    return pl.pallas_call(
        functools.partial(totals_kernel, scale),
        in_specs=[pl.BlockSpec(memory_space=pltpu.VMEM)],
        out_specs=[
            pl.BlockSpec(memory_space=pltpu.VMEM),
            pl.BlockSpec(memory_space=pltpu.SMEM),
        ],
        out_shape=[
            jax.ShapeDtypeStruct((DOM_DEV, 64), F32),
            jax.ShapeDtypeStruct((2,), F32),
        ],
        compiler_params=pltpu.CompilerParams(vmem_limit_bytes=16 << 20),
        name="totals",
    )(gathered)


def per_device(density, col_index, counts, domain):
    per_dev, capacity, width = density.shape[:3]
    block_rows = col_index.shape[0]
    radius = (capacity - 1) // 2
    slabs = lax.axis_size("rows")
    devices = slabs * lax.axis_size("layer")
    start = lax.axis_index("rows") * per_dev

    columns = lax.dynamic_slice_in_dim(col_index.T, start, per_dev, 1)
    row_ids = start + jnp.arange(per_dev, dtype=jnp.int32)
    offset = (columns - row_ids[None, :] + radius) % block_rows
    lane = jnp.arange(40, dtype=jnp.int32)
    slots = jnp.arange(capacity, dtype=jnp.int32)
    meta = jnp.sum(
        jnp.where(offset.T[:, :, None] == lane[None, None, :], slots[None, :, None], 0), axis=1
    )

    def device(row, core):
        return (row % slabs) * 2 + core

    ahead = [(device(r, 0), device(r + 1, 0)) for r in range(slabs)]
    ahead += [(device(r, 1), device(r - 1, 1)) for r in range(slabs)]
    across = [(device(r, c), device(r, 1 - c)) for r in range(slabs) for c in range(2)]

    (ss,) = pack(((SYM, 1, 1),), meta, density)
    ms, mm = pack(((FULL, 0, 1), (SYM, 0, 0)), meta, density, ss)
    partial, mine = diagonals(meta, domain, density, mm, devices)
    ss = lax.ppermute(ss, AXES, ahead)
    ms = lax.ppermute(ms, AXES, ahead)
    mm = lax.ppermute(mm, AXES, ahead)
    gathered = lax.all_to_all(partial, AXES, 0, 0, tiled=True)
    part, near = local(meta, density, mine, partial)
    corner = lax.ppermute(ss, AXES, across)
    square, first = most(meta, counts, (mine, part, near), (ss, ms, corner), capacity)
    square = last(meta, counts, first, mine, mm, square)

    populations, traces = totals(gathered, 1.0 / (block_rows * width))
    return (square, populations, traces)


def solution(mesh):
    placed = (P("rows", None, None, None), P(), P(), P())
    return jax.shard_map(
        per_device,
        mesh=mesh,
        in_specs=placed,
        out_specs=(P(("rows", "layer"), None, None, None), P(("rows", "layer"), None), P()),
        check_vma=False,
    )
```

```python
import functools

import jax
import jax.numpy as jnp
from jax import lax
from jax.experimental import pallas as pl
from jax.experimental.pallas import tpu as pltpu
from jax.sharding import PartitionSpec as P


DOM_DEV = 2
AXES = ("rows", "layer")
SYM = [(u, t) for u in range(4) for t in range(u, 4)]
FULL = [(u, t) for u in range(4) for t in range(4)]
NT = (((1,), (1,)), ((), ()))
BF = jnp.bfloat16
F32 = jnp.float32
EVERY = pl.ds(0, 512)
IN_HBM = pl.BlockSpec(memory_space=pltpu.HBM)


def issue(groups, meta, density, buf, sems):
    layer = lax.axis_index("layer")
    starts = (8 * layer, 8 * (1 - layer))
    base = 0
    for g, (tiles, near, far) in enumerate(groups):
        row, col = starts[near], starts[far]
        for n, (u, t) in enumerate(tiles):
            for r in range(2):
                for s in range(2):
                    k = row + 2 * u + r
                    slot = meta[k, (col - row) + 2 * t + s - 2 * u - r + 16]
                    at = base + 4 * n + 2 * r + s
                    pltpu.make_async_copy(density.at[k, slot], buf.at[at], sems.at[g]).start()
        base += 4 * len(tiles)


def collect(groups, outs, buf, sems):
    base = 0
    for g, (tiles, _, _) in enumerate(groups):
        span = buf.at[pl.ds(base, 4 * len(tiles))]
        pltpu.make_async_copy(span, span, sems.at[g]).wait()
        for n in range(len(tiles)):
            for r in range(2):
                at = base + 4 * n + 2 * r
                outs[g][n, 64 * r : 64 * r + 64, :] = jnp.concatenate(
                    [buf[at], buf[at + 1]], axis=1
                )
        base += 4 * len(tiles)


def pack_kernel(groups, meta, density, *rest):
    outs, buf, sems = rest[: len(groups)], rest[-2], rest[-1]
    issue(groups, meta, density, buf, sems)
    collect(groups, outs, buf, sems)


def pack(groups, meta, density):
    sizes = [len(tiles) for tiles, _, _ in groups]
    return pl.pallas_call(
        functools.partial(pack_kernel, groups),
        grid_spec=pltpu.PrefetchScalarGridSpec(
            num_scalar_prefetch=1,
            grid=(1,),
            in_specs=[IN_HBM],
            out_specs=[pl.BlockSpec((n, 128, 128), lambda i, m: (0, 0, 0)) for n in sizes],
            scratch_shapes=[
                pltpu.VMEM((4 * sum(sizes), 64, 64), BF),
                pltpu.SemaphoreType.DMA((len(sizes),)),
            ],
        ),
        out_shape=[jax.ShapeDtypeStruct((n, 128, 128), BF) for n in sizes],
        compiler_params=pltpu.CompilerParams(vmem_limit_bytes=16 << 20),
        cost_estimate=pl.CostEstimate(
            flops=0, bytes_accessed=sum(sizes) << 17, transcendentals=0
        ),
        name="pack",
    )(meta, density)


def rest_kernel(groups, meta, domain, density, _, *rest):
    outs, out_ref = rest[: len(groups)], rest[len(groups)]
    buf, packed, rows_ref, sems, sums = rest[len(groups) + 1 :]
    layer = lax.axis_index("layer")
    start = 16 * lax.axis_index("rows")
    base = 8 * layer
    issue(groups, meta, density, buf, packed)
    for i in range(4):
        source = density.at[pl.ds(base + 2 * i, 2)]
        pltpu.make_async_copy(source, rows_ref.at[pl.ds(2 * i, 2)], sems.at[i]).start()
    out_ref[...] = jnp.zeros_like(out_ref)
    sums[...] = jnp.zeros_like(sums)
    eye = lax.broadcasted_iota(jnp.int32, (64, 64), 0) == lax.broadcasted_iota(
        jnp.int32, (64, 64), 1
    )
    sub = lax.broadcasted_iota(jnp.int32, (8, 64), 0)
    collect(groups, outs, buf, packed)

    @pl.loop(0, 4)
    def _(u):
        pltpu.make_async_copy(
            density.at[pl.ds(0, 2)], rows_ref.at[pl.ds(2 * u, 2)], sems.at[u]
        ).wait()
        for r in range(2):
            i = 2 * u + r
            k = base + i
            total = jnp.zeros((64, 64), F32)
            for s in range(rows_ref.shape[1]):
                block = rows_ref[i, s].astype(F32)
                total += block * block
            column = jnp.sum(total, axis=1, keepdims=True)
            squares = jnp.sum(jnp.where(eye, column, 0.0), axis=0, keepdims=True)
            squares = squares.astype(BF).astype(F32)
            middle = rows_ref[i, meta[k, 16]].astype(F32)
            diagonal = jnp.sum(jnp.where(eye, middle, 0.0), axis=0, keepdims=True)
            target = domain[start + k]
            owner = target // DOM_DEV
            place = target - owner * DOM_DEV
            out_ref[owner, :, 0:64] = out_ref[owner, :, 0:64] + jnp.where(
                sub == place, squares, 0.0
            )
            sums[:, 0:64] = sums[:, 0:64] + jnp.where(
                sub == DOM_DEV, diagonal, jnp.where(sub == DOM_DEV + 1, squares, 0.0)
            )

    out_ref[...] = out_ref[...] + sums[...][None]


def rest(groups, meta, domain, density, after, devices):
    capacity = density.shape[1]
    sizes = [len(tiles) for tiles, _, _ in groups]
    shapes = [(n, 128, 128) for n in sizes] + [(devices, 8, 128)]
    return pl.pallas_call(
        functools.partial(rest_kernel, groups),
        grid_spec=pltpu.PrefetchScalarGridSpec(
            num_scalar_prefetch=2,
            grid=(1,),
            in_specs=[IN_HBM, IN_HBM],
            out_specs=[pl.BlockSpec(shape, lambda i, m, d: (0, 0, 0)) for shape in shapes],
            scratch_shapes=[
                pltpu.VMEM((4 * sum(sizes), 64, 64), BF),
                pltpu.SemaphoreType.DMA((len(sizes),)),
                pltpu.VMEM((8, capacity, 64, 64), BF),
                pltpu.SemaphoreType.DMA((4,)),
                pltpu.VMEM((8, 128), F32),
            ],
        ),
        out_shape=[
            jax.ShapeDtypeStruct(shape, F32 if n == len(sizes) else BF)
            for n, shape in enumerate(shapes)
        ],
        compiler_params=pltpu.CompilerParams(vmem_limit_bytes=16 << 20),
        cost_estimate=pl.CostEstimate(flops=0, bytes_accessed=8 << 20, transcendentals=0),
        name="rest",
    )(meta, domain, density, after)


def spread(slots, block, own, first, at, k):
    zero = jnp.zeros((64, 64), BF)
    for r in range(2):
        rows = pl.ds(pl.multiple_of(at + 64 * r, 64), 64)
        for pp in range(17):
            halves = []
            for s in range(2):
                d = 2 * pp + s - r
                halves.append(block(r, slots[k + r, d]) if 0 <= d <= 32 else zero)
            own[first + pp, rows, :] = jnp.concatenate(halves, axis=1)


def octant(layer, q):
    return jnp.where(layer == 0, q, 5 - q)


def wide(ref, pair, rows):
    return jnp.concatenate([ref[pair, rows, :], ref[pair + 1, rows, :]], axis=1)


def local_kernel(meta, counts, density, _, head_ref, rest_ref, part_ref, out_ref, *scratch):
    rows_ref, sems, mine, other, near_ref, stage, sent = scratch
    layer = lax.axis_index("layer")
    base = 8 * layer
    sib = 8 * (1 - layer)
    for n in range(8):
        source = density.at[pl.ds((base if n < 4 else sib) + 2 * (n % 4), 2)]
        pltpu.make_async_copy(source, rows_ref.at[pl.ds(2 * n, 2)], sems.at[n]).start()

    @pl.loop(0, 24)
    def _(p):
        mine[p] = jnp.zeros(mine.shape[1:], BF)
        other[p] = jnp.zeros(other.shape[1:], BF)

    def gather(u, own, first, at, k):
        pltpu.make_async_copy(
            density.at[pl.ds(0, 2)], rows_ref.at[pl.ds(2 * u, 2)], sems.at[u]
        ).wait()
        spread(meta, lambda r, slot: rows_ref[2 * u + r, slot], own, first, at, k)

    @pl.loop(0, 4)
    def _(u):
        gather(u, mine, 4 * layer + u, 128 * u, base + 2 * u)

    at = [4 * octant(layer, q) for q in range(5)]
    every = pl.ds(0, 512)

    def put(ref, base, half, value):
        ref[base + 2 * half] = value[:, 0:128].astype(ref.dtype)
        ref[base + 2 * half + 1] = value[:, 128:256].astype(ref.dtype)

    def left(ref, octs, rows):
        return jnp.concatenate(
            [wide(ref, at[q] + 2 * h, rows) for q in octs for h in range(2)], axis=1
        )

    def own(base, octs, source):
        for half in range(2):
            right = left(source, octs, pl.ds(256 * half, 256))
            value = lax.dot_general(left(mine, octs, every), right, NT, preferred_element_type=F32)
            put(near_ref, base, half, value)

    def toward(ref, base, q, octs):
        for half in range(2):
            right = jnp.concatenate(
                [wide((mine, other)[o - 2], at[q] + 2 * half, every) for o in octs], axis=0
            )
            value = jnp.dot(left(mine, octs, every), right, preferred_element_type=F32)
            put(ref, base, half, value)

    for p in range(4):
        head_ref[p] = mine[at[0] + p]
        rest_ref[p] = mine[at[1] + p]
        rest_ref[4 + p] = mine[at[4] + p]

    def emit(base, first):
        for i in range(8):
            for e in range(8):
                n = 8 * base + 8 * i + e
                block = lane_half(near_ref, base // 2 + e // 2, pl.ds(64 * i, 64), e % 2)
                place_block(meta, counts, i, first + e, block, stage.at[n], out_ref, sent)

    own(0, (0, 1, 2, 3, 4), mine)
    emit(0, 16)
    toward(part_ref, 0, 0, (2,))

    @pl.loop(0, 4)
    def _(u):
        gather(u + 4, other, 4 * (1 - layer) + u, 128 * u, sib + 2 * u)

    own(4, (1, 2, 3, 4), other)
    emit(8, jnp.where(layer == 0, 24, 8))
    toward(part_ref, 4, 1, (2, 3))
    toward(part_ref, 8, 4, (2, 3))
    pltpu.make_async_copy(stage, stage, sent).wait()


def whole(*shape):
    return pl.BlockSpec(shape, lambda i, m, c: (0, 0, 0))


def local(meta, counts, density, after):
    capacity = density.shape[1]
    parts = ((4, BF), (8, BF), (12, F32))
    return pl.pallas_call(
        local_kernel,
        grid_spec=pltpu.PrefetchScalarGridSpec(
            num_scalar_prefetch=2,
            grid=(1,),
            in_specs=[IN_HBM, IN_HBM],
            out_specs=[whole(n, 512, 128) for n, _ in parts] + [IN_HBM],
            scratch_shapes=[
                pltpu.VMEM((16, capacity, 64, 64), BF),
                pltpu.SemaphoreType.DMA((8,)),
                pltpu.VMEM((24, 512, 128), BF),
                pltpu.VMEM((24, 512, 128), BF),
                pltpu.VMEM((8, 512, 128), BF),
                pltpu.VMEM((128, 64, 64), BF),
                pltpu.SemaphoreType.DMA,
            ],
        ),
        out_shape=[jax.ShapeDtypeStruct((n, 512, 128), t) for n, t in parts]
        + [jax.ShapeDtypeStruct((8, capacity, 64, 64), BF)],
        compiler_params=pltpu.CompilerParams(vmem_limit_bytes=36 << 20),
        cost_estimate=pl.CostEstimate(
            flops=4 << 30, bytes_accessed=16 << 20, transcendentals=0
        ),
        name="local",
    )(meta, counts, density, after)


def beside(tiles, base, count):
    return jnp.concatenate([tiles[base + n] for n in range(count)], axis=1)


def corners(tiles_ref):
    tile = {ut: tiles_ref[n] for n, ut in enumerate(SYM)}

    def square(u):
        top = jnp.concatenate([tile[u, u], tile[u, u + 1]], axis=1)
        bottom = jnp.concatenate([tile[u, u + 1].T, tile[u + 1, u + 1]], axis=1)
        return jnp.concatenate([top, bottom], axis=0)

    cross = jnp.concatenate(
        [jnp.concatenate([tile[u, 2], tile[u, 3]], axis=1) for u in range(2)], axis=0
    )
    return square(0), cross, square(2)


def product(ref, base, tiles_ref):
    upper, cross, lower = corners(tiles_ref)
    low, high = wide(ref, base, EVERY), wide(ref, base + 2, EVERY)
    yield 0, jnp.dot(low, upper, preferred_element_type=F32) + lax.dot_general(
        high, cross, NT, preferred_element_type=F32
    )
    yield 1, jnp.dot(
        jnp.concatenate([low, high], axis=1),
        jnp.concatenate([cross, lower], axis=0),
        preferred_element_type=F32,
    )


def lane_half(ref, pair, rows, odd):
    return ref[pair, rows, :][:, 64 * odd : 64 * odd + 64]


def place_block(meta, counts, i, c, block, stage, out_ref, sem):
    k = 8 * lax.axis_index("layer") + i
    slot = meta[k, c - i]
    live = slot < counts[16 * lax.axis_index("rows") + k]
    stage[...] = jnp.where(live, block, jnp.zeros_like(block))
    pltpu.make_async_copy(stage, out_ref.at[i, slot], sem).start()


def finish(ref, at, partial, base, half, value):
    for s in range(2):
        p = 2 * half + s
        total = partial[base + p] + value[:, 128 * s : 128 * s + 128]
        ref[at + p] = total.astype(ref.dtype)


def emit_edge(core, near, meta, counts, ref, stage, at, out_ref, sem):
    above = near == (core == 1)
    n = at
    for i in range(8):
        for e in range(i, 8) if above else range(i + 1):
            block = lane_half(ref, e // 2, pl.ds(64 * i, 64), e % 2)
            c = e if above else 32 + e
            place_block(meta, counts, i, c, block, stage.at[n], out_ref, sem)
            n += 1


def middle_kernel(
    meta, counts, head, others, part, ss, ms, corner, _, first_ref, out_ref, y, middle, stage, sem
):
    layer = lax.axis_index("layer")
    upper, cross, lower = corners(ss)
    high = jnp.concatenate([wide(others, 0, EVERY), wide(others, 2, EVERY)], axis=1)
    low = jnp.concatenate([wide(head, 0, EVERY), wide(head, 2, EVERY)], axis=1)
    for half in range(2):
        top = jnp.concatenate([beside(ms, 4 * u + 2 * half, 2) for u in range(4)], axis=0)
        value = jnp.dot(low, top, preferred_element_type=F32)
        if half:
            right = jnp.concatenate([cross, lower], axis=0)
            value += jnp.dot(high, right, preferred_element_type=F32)
        else:
            value += jnp.dot(high[:, 0:256], upper, preferred_element_type=F32)
            value += lax.dot_general(high[:, 256:512], cross, NT, preferred_element_type=F32)
        finish(middle, 0, part, 4, half, value)

    for i in range(8):
        for e in range(8):
            block = lane_half(middle, e // 2, pl.ds(64 * i, 64), e % 2)
            c = jnp.where(layer == 0, 8, 24) + e
            place_block(meta, counts, i, c, block, stage.at[8 * i + e], out_ref, sem)

    for half, value in product(others, 4, corner):
        finish(y, 0, part, 8, half, value)
    for core in range(2):
        pl.when(layer == core)(
            lambda core=core: emit_edge(core, True, meta, counts, y, stage, 64, out_ref, sem)
        )
    for half in range(2):
        right = jnp.concatenate([beside(ms, 4 * u, 4) for u in (2 * half, 2 * half + 1)], axis=0)
        value = lax.dot_general(high, right, NT, preferred_element_type=F32)
        finish(first_ref, 0, part, 0, half, value)
    pltpu.make_async_copy(stage, stage, sem).wait()


def last_kernel(meta, counts, head, first, mm, _, out_ref, y, stage, sem):
    layer = lax.axis_index("layer")
    for half, value in product(head, 0, mm):
        finish(y, 0, first, 0, half, value)
    for core in range(2):
        pl.when(layer == core)(
            lambda core=core: emit_edge(core, False, meta, counts, y, stage, 0, out_ref, sem)
        )
    pltpu.make_async_copy(stage, stage, sem).wait()


def closing(kernel, meta, counts, inputs, square, blocks, extra, buffers, limit):
    scratch = [pltpu.VMEM((4, 512, 128), BF)] * buffers
    return pl.pallas_call(
        kernel,
        grid_spec=pltpu.PrefetchScalarGridSpec(
            num_scalar_prefetch=2,
            grid=(1,),
            in_specs=[whole(*x.shape) for x in inputs] + [IN_HBM],
            out_specs=[whole(*x.shape) for x in extra] + [IN_HBM],
            scratch_shapes=scratch + [pltpu.VMEM((blocks, 64, 64), BF), pltpu.SemaphoreType.DMA],
        ),
        out_shape=[*extra, jax.ShapeDtypeStruct(square.shape, BF)],
        input_output_aliases={2 + len(inputs): len(extra)},
        compiler_params=pltpu.CompilerParams(vmem_limit_bytes=limit << 20),
        cost_estimate=pl.CostEstimate(
            flops=len(inputs) << 27, bytes_accessed=6 << 20, transcendentals=0
        ),
    )(meta, counts, *inputs, square)


def totals_kernel(scale, sent, _, populations_ref, traces_ref):
    total = jnp.sum(sent[...], axis=0)[:, 0:64]
    populations_ref[...] = total[0:DOM_DEV]
    for n in range(2):
        traces_ref[n] = jnp.sum(total[DOM_DEV + n : DOM_DEV + n + 1]) * scale


def totals(gathered, after, scale):
    return pl.pallas_call(
        functools.partial(totals_kernel, scale),
        in_specs=[pl.BlockSpec(memory_space=pltpu.VMEM), IN_HBM],
        out_specs=[
            pl.BlockSpec(memory_space=pltpu.VMEM),
            pl.BlockSpec(memory_space=pltpu.SMEM),
        ],
        out_shape=[
            jax.ShapeDtypeStruct((DOM_DEV, 64), F32),
            jax.ShapeDtypeStruct((2,), F32),
        ],
        compiler_params=pltpu.CompilerParams(vmem_limit_bytes=16 << 20),
        name="totals",
    )(gathered, after)


def in_hbm(value):
    return pltpu.with_memory_space_constraint(value, pltpu.HBM)


def per_device(density, col_index, counts, domain):
    per_dev, capacity, width = density.shape[:3]
    block_rows = col_index.shape[0]
    radius = (capacity - 1) // 2
    slabs = lax.axis_size("rows")
    devices = slabs * lax.axis_size("layer")
    start = lax.axis_index("rows") * per_dev

    columns = lax.dynamic_slice_in_dim(col_index.T, start, per_dev, 1)
    row_ids = start + jnp.arange(per_dev, dtype=jnp.int32)
    offset = (columns - row_ids[None, :] + radius) % block_rows
    lane = jnp.arange(40, dtype=jnp.int32)
    slots = jnp.arange(capacity, dtype=jnp.int32)
    meta = jnp.sum(
        jnp.where(offset.T[:, :, None] == lane[None, None, :], slots[None, :, None], 0), axis=1
    )

    def device(row, core):
        return (row % slabs) * 2 + core

    ahead = [(device(r, 0), device(r + 1, 0)) for r in range(slabs)]
    ahead += [(device(r, 1), device(r - 1, 1)) for r in range(slabs)]
    across = [(device(r, c), device(r, 1 - c)) for r in range(slabs) for c in range(2)]

    density = in_hbm(density)
    (ss,) = pack(((SYM, 1, 1),), meta, density)
    tiles = ((FULL, 0, 1), (SYM, 0, 0))
    ms, mm, partial = rest(tiles, meta, domain, density, ss, devices)
    ss = lax.ppermute(ss, AXES, ahead)
    ms = lax.ppermute(ms, AXES, ahead)
    mm = lax.ppermute(mm, AXES, ahead)
    gathered = lax.all_to_all(partial, AXES, 0, 0, tiled=True)
    head, others, part, square = local(meta, counts, density, partial)
    corner = lax.ppermute(ss, AXES, across)
    inputs = (head, others, part, ss, ms, corner)
    extra = (jax.ShapeDtypeStruct(head.shape, F32),)
    first, square = closing(middle_kernel, meta, counts, inputs, in_hbm(square), 100, extra, 2, 24)
    inputs = (head, first, mm)
    (square,) = closing(last_kernel, meta, counts, inputs, in_hbm(square), 36, (), 1, 16)
    populations, traces = totals(gathered, in_hbm(square), 1.0 / (block_rows * width))
    return (square, populations, traces)


def solution(mesh):
    placed = (P("rows", None, None, None), P(), P(), P())
    return jax.shard_map(
        per_device,
        mesh=mesh,
        in_specs=placed,
        out_specs=(P(("rows", "layer"), None, None, None), P(("rows", "layer"), None), P()),
        check_vma=False,
    )
```

```python
import functools

import jax
import jax.numpy as jnp
from jax import lax
from jax.experimental import pallas as pl
from jax.experimental.pallas import tpu as pltpu
from jax.sharding import PartitionSpec as P


DOM_DEV = 2
AXES = ("rows", "layer")


def tile_blocks(u, t):
    return [(2 * u + r, 2 * t + s) for r in range(2) for s in range(2)]


OFF = [(u, t) for u in range(4) for t in range(u + 1, 4)]
DIAGONAL = [
    [(0, 0), (0, 1), (2, 2), (2, 3)],
    [(4, 4), (4, 5), (6, 6), (6, 7)],
    [(1, 1), (3, 3), (5, 5), (7, 7)],
]
SYM = [tile_blocks(u, t) for u, t in OFF] + DIAGONAL
FULL = [tile_blocks(u, t) for u in range(4) for t in range(4)]
NT = (((1,), (1,)), ((), ()))
BF = jnp.bfloat16
F32 = jnp.float32
EVERY = pl.ds(0, 512)
IN_HBM = pl.BlockSpec(memory_space=pltpu.HBM)


def issue(groups, meta, density, buf, sems):
    layer = lax.axis_index("layer")
    starts = (8 * layer, 8 * (1 - layer))
    base = 0
    for g, (tiles, near, far) in enumerate(groups):
        row, col = starts[near], starts[far]
        for n, blocks in enumerate(tiles):
            for x, (i, j) in enumerate(blocks):
                slot = meta[row + i, (col - row) + j - i + 16]
                source = density.at[row + i, slot]
                pltpu.make_async_copy(source, buf.at[base + 4 * n + x], sems.at[g]).start()
        base += 4 * len(tiles)


def collect(groups, outs, buf, sems):
    base = 0
    for g, (tiles, _, _) in enumerate(groups):
        span = buf.at[pl.ds(base, 4 * len(tiles))]
        pltpu.make_async_copy(span, span, sems.at[g]).wait()
        for n in range(len(tiles)):
            for r in range(2):
                at = base + 4 * n + 2 * r
                outs[g][n, 64 * r : 64 * r + 64, :] = jnp.concatenate(
                    [buf[at], buf[at + 1]], axis=1
                )
        base += 4 * len(tiles)


def pack_kernel(groups, meta, density, *rest):
    outs, buf, sems = rest[: len(groups)], rest[-2], rest[-1]
    issue(groups, meta, density, buf, sems)
    collect(groups, outs, buf, sems)


def pack(groups, meta, density):
    sizes = [len(tiles) for tiles, _, _ in groups]
    return pl.pallas_call(
        functools.partial(pack_kernel, groups),
        grid_spec=pltpu.PrefetchScalarGridSpec(
            num_scalar_prefetch=1,
            grid=(1,),
            in_specs=[IN_HBM],
            out_specs=[pl.BlockSpec((n, 128, 128), lambda i, m: (0, 0, 0)) for n in sizes],
            scratch_shapes=[
                pltpu.VMEM((4 * sum(sizes), 64, 64), BF),
                pltpu.SemaphoreType.DMA((len(sizes),)),
            ],
        ),
        out_shape=[jax.ShapeDtypeStruct((n, 128, 128), BF) for n in sizes],
        compiler_params=pltpu.CompilerParams(vmem_limit_bytes=16 << 20),
        cost_estimate=pl.CostEstimate(
            flops=0, bytes_accessed=sum(sizes) << 17, transcendentals=0
        ),
        name="pack",
    )(meta, density)


def rest_kernel(groups, meta, domain, density, _, *rest):
    outs, out_ref = rest[: len(groups)], rest[len(groups)]
    buf, packed, rows_ref, sems, sums = rest[len(groups) + 1 :]
    layer = lax.axis_index("layer")
    start = 16 * lax.axis_index("rows")
    base = 8 * layer
    issue(groups, meta, density, buf, packed)
    for i in range(4):
        source = density.at[pl.ds(base + 2 * i, 2)]
        pltpu.make_async_copy(source, rows_ref.at[pl.ds(2 * i, 2)], sems.at[i]).start()
    out_ref[...] = jnp.zeros_like(out_ref)
    sums[...] = jnp.zeros_like(sums)
    eye = lax.broadcasted_iota(jnp.int32, (64, 64), 0) == lax.broadcasted_iota(
        jnp.int32, (64, 64), 1
    )
    sub = lax.broadcasted_iota(jnp.int32, (8, 64), 0)
    collect(groups, outs, buf, packed)

    @pl.loop(0, 4)
    def _(u):
        pltpu.make_async_copy(
            density.at[pl.ds(0, 2)], rows_ref.at[pl.ds(2 * u, 2)], sems.at[u]
        ).wait()
        for r in range(2):
            i = 2 * u + r
            k = base + i
            total = jnp.zeros((64, 64), F32)
            for s in range(rows_ref.shape[1]):
                block = rows_ref[i, s].astype(F32)
                total += block * block
            column = jnp.sum(total, axis=1, keepdims=True)
            squares = jnp.sum(jnp.where(eye, column, 0.0), axis=0, keepdims=True)
            squares = squares.astype(BF).astype(F32)
            middle = rows_ref[i, meta[k, 16]].astype(F32)
            diagonal = jnp.sum(jnp.where(eye, middle, 0.0), axis=0, keepdims=True)
            target = domain[start + k]
            owner = target // DOM_DEV
            place = target - owner * DOM_DEV
            out_ref[owner, :, 0:64] = out_ref[owner, :, 0:64] + jnp.where(
                sub == place, squares, 0.0
            )
            sums[:, 0:64] = sums[:, 0:64] + jnp.where(
                sub == DOM_DEV, diagonal, jnp.where(sub == DOM_DEV + 1, squares, 0.0)
            )

    out_ref[...] = out_ref[...] + sums[...][None]


def rest(groups, meta, domain, density, after, devices):
    capacity = density.shape[1]
    sizes = [len(tiles) for tiles, _, _ in groups]
    shapes = [(n, 128, 128) for n in sizes] + [(devices, 8, 128)]
    return pl.pallas_call(
        functools.partial(rest_kernel, groups),
        grid_spec=pltpu.PrefetchScalarGridSpec(
            num_scalar_prefetch=2,
            grid=(1,),
            in_specs=[IN_HBM, IN_HBM],
            out_specs=[pl.BlockSpec(shape, lambda i, m, d: (0, 0, 0)) for shape in shapes],
            scratch_shapes=[
                pltpu.VMEM((4 * sum(sizes), 64, 64), BF),
                pltpu.SemaphoreType.DMA((len(sizes),)),
                pltpu.VMEM((8, capacity, 64, 64), BF),
                pltpu.SemaphoreType.DMA((4,)),
                pltpu.VMEM((8, 128), F32),
            ],
        ),
        out_shape=[
            jax.ShapeDtypeStruct(shape, F32 if n == len(sizes) else BF)
            for n, shape in enumerate(shapes)
        ],
        compiler_params=pltpu.CompilerParams(vmem_limit_bytes=16 << 20),
        cost_estimate=pl.CostEstimate(flops=0, bytes_accessed=8 << 20, transcendentals=0),
        name="rest",
    )(meta, domain, density, after)


def spread(slots, block, own, first, at, k):
    zero = jnp.zeros((64, 64), BF)
    for r in range(2):
        rows = pl.ds(pl.multiple_of(at + 64 * r, 64), 64)
        for pp in range(17):
            halves = []
            for s in range(2):
                d = 2 * pp + s - r
                halves.append(block(r, slots[k + r, d]) if 0 <= d <= 32 else zero)
            own[first + pp, rows, :] = jnp.concatenate(halves, axis=1)


def octant(layer, q):
    return jnp.where(layer == 0, q, 5 - q)


def wide(ref, pair, rows):
    return jnp.concatenate([ref[pair, rows, :], ref[pair + 1, rows, :]], axis=1)


def local_kernel(meta, counts, density, _, head_ref, rest_ref, part_ref, out_ref, *scratch):
    rows_ref, sems, mine, other, near_ref, stage, sent = scratch
    layer = lax.axis_index("layer")
    base = 8 * layer
    sib = 8 * (1 - layer)
    for n in range(8):
        source = density.at[pl.ds((base if n < 4 else sib) + 2 * (n % 4), 2)]
        pltpu.make_async_copy(source, rows_ref.at[pl.ds(2 * n, 2)], sems.at[n]).start()

    @pl.loop(0, 24)
    def _(p):
        mine[p] = jnp.zeros(mine.shape[1:], BF)
        other[p] = jnp.zeros(other.shape[1:], BF)

    def gather(u, own, first, at, k):
        pltpu.make_async_copy(
            density.at[pl.ds(0, 2)], rows_ref.at[pl.ds(2 * u, 2)], sems.at[u]
        ).wait()
        spread(meta, lambda r, slot: rows_ref[2 * u + r, slot], own, first, at, k)

    @pl.loop(0, 4)
    def _(u):
        gather(u, mine, 4 * layer + u, 128 * u, base + 2 * u)

    at = [4 * octant(layer, q) for q in range(5)]
    every = pl.ds(0, 512)

    def put(ref, base, half, value):
        ref[base + 2 * half] = value[:, 0:128].astype(ref.dtype)
        ref[base + 2 * half + 1] = value[:, 128:256].astype(ref.dtype)

    def left(ref, octs, rows):
        return jnp.concatenate(
            [wide(ref, at[q] + 2 * h, rows) for q in octs for h in range(2)], axis=1
        )

    def own(base, octs, source):
        for half in range(2):
            right = left(source, octs, pl.ds(256 * half, 256))
            value = lax.dot_general(left(mine, octs, every), right, NT, preferred_element_type=F32)
            put(near_ref, base, half, value)

    def toward(ref, base, q, octs):
        for half in range(2):
            right = jnp.concatenate(
                [wide((mine, other)[o - 2], at[q] + 2 * half, every) for o in octs], axis=0
            )
            value = jnp.dot(left(mine, octs, every), right, preferred_element_type=F32)
            put(ref, base, half, value)

    for p in range(4):
        head_ref[p] = mine[at[0] + p]
        rest_ref[p] = mine[at[1] + p]
        rest_ref[4 + p] = mine[at[4] + p]

    def emit(base, first):
        for i in range(8):
            for e in range(8):
                n = 8 * base + 8 * i + e
                block = lane_half(near_ref, base // 2 + e // 2, pl.ds(64 * i, 64), e % 2)
                place_block(meta, counts, i, first + e, block, stage.at[n], out_ref, sent)

    own(0, (0, 1, 2, 3, 4), mine)
    emit(0, 16)
    toward(part_ref, 0, 0, (2,))

    @pl.loop(0, 4)
    def _(u):
        gather(u + 4, other, 4 * (1 - layer) + u, 128 * u, sib + 2 * u)

    own(4, (1, 2, 3, 4), other)
    emit(8, jnp.where(layer == 0, 24, 8))
    toward(part_ref, 4, 1, (2, 3))
    toward(part_ref, 8, 4, (2, 3))
    pltpu.make_async_copy(stage, stage, sent).wait()


def whole(*shape):
    return pl.BlockSpec(shape, lambda i, m, c: (0, 0, 0))


def local(meta, counts, density, after):
    capacity = density.shape[1]
    parts = ((4, BF), (8, BF), (12, F32))
    return pl.pallas_call(
        local_kernel,
        grid_spec=pltpu.PrefetchScalarGridSpec(
            num_scalar_prefetch=2,
            grid=(1,),
            in_specs=[IN_HBM, IN_HBM],
            out_specs=[whole(n, 512, 128) for n, _ in parts] + [IN_HBM],
            scratch_shapes=[
                pltpu.VMEM((16, capacity, 64, 64), BF),
                pltpu.SemaphoreType.DMA((8,)),
                pltpu.VMEM((24, 512, 128), BF),
                pltpu.VMEM((24, 512, 128), BF),
                pltpu.VMEM((8, 512, 128), BF),
                pltpu.VMEM((128, 64, 64), BF),
                pltpu.SemaphoreType.DMA,
            ],
        ),
        out_shape=[jax.ShapeDtypeStruct((n, 512, 128), t) for n, t in parts]
        + [jax.ShapeDtypeStruct((8, capacity, 64, 64), BF)],
        compiler_params=pltpu.CompilerParams(vmem_limit_bytes=36 << 20),
        cost_estimate=pl.CostEstimate(
            flops=4 << 30, bytes_accessed=16 << 20, transcendentals=0
        ),
        name="local",
    )(meta, counts, density, after)


def beside(tiles, base, count):
    return jnp.concatenate([tiles[base + n] for n in range(count)], axis=1)


def corners(tiles_ref):
    tile = {ut: tiles_ref[n] for n, ut in enumerate(OFF)}
    for u in range(4):
        top = tiles_ref[6 + u // 2, 64 * (u % 2) : 64 * (u % 2) + 64, :]
        below = tiles_ref[8, 64 * (u // 2) : 64 * (u // 2) + 64, :]
        below = below[:, 64 * (u % 2) : 64 * (u % 2) + 64]
        bottom = jnp.concatenate([top[:, 64:128].T, below], axis=1)
        tile[u, u] = jnp.concatenate([top, bottom], axis=0)

    def square(u):
        top = jnp.concatenate([tile[u, u], tile[u, u + 1]], axis=1)
        bottom = jnp.concatenate([tile[u, u + 1].T, tile[u + 1, u + 1]], axis=1)
        return jnp.concatenate([top, bottom], axis=0)

    cross = jnp.concatenate(
        [jnp.concatenate([tile[u, 2], tile[u, 3]], axis=1) for u in range(2)], axis=0
    )
    return square(0), cross, square(2)


def product(ref, base, tiles_ref):
    upper, cross, lower = corners(tiles_ref)
    low, high = wide(ref, base, EVERY), wide(ref, base + 2, EVERY)
    yield 0, jnp.dot(low, upper, preferred_element_type=F32) + lax.dot_general(
        high, cross, NT, preferred_element_type=F32
    )
    yield 1, jnp.dot(
        jnp.concatenate([low, high], axis=1),
        jnp.concatenate([cross, lower], axis=0),
        preferred_element_type=F32,
    )


def lane_half(ref, pair, rows, odd):
    return ref[pair, rows, :][:, 64 * odd : 64 * odd + 64]


def place_block(meta, counts, i, c, block, stage, out_ref, sem):
    k = 8 * lax.axis_index("layer") + i
    slot = meta[k, c - i]
    live = slot < counts[16 * lax.axis_index("rows") + k]
    stage[...] = jnp.where(live, block, jnp.zeros_like(block))
    pltpu.make_async_copy(stage, out_ref.at[i, slot], sem).start()


def finish(ref, at, partial, base, half, value):
    for s in range(2):
        p = 2 * half + s
        total = partial[base + p] + value[:, 128 * s : 128 * s + 128]
        ref[at + p] = total.astype(ref.dtype)


def emit_edge(core, near, meta, counts, ref, stage, at, out_ref, sem):
    above = near == (core == 1)
    n = at
    for i in range(8):
        for e in range(i, 8) if above else range(i + 1):
            block = lane_half(ref, e // 2, pl.ds(64 * i, 64), e % 2)
            c = e if above else 32 + e
            place_block(meta, counts, i, c, block, stage.at[n], out_ref, sem)
            n += 1


def middle_kernel(
    meta, counts, head, others, part, ss, ms, corner, _, first_ref, out_ref, y, middle, stage, sem
):
    layer = lax.axis_index("layer")
    upper, cross, lower = corners(ss)
    high = jnp.concatenate([wide(others, 0, EVERY), wide(others, 2, EVERY)], axis=1)
    low = jnp.concatenate([wide(head, 0, EVERY), wide(head, 2, EVERY)], axis=1)
    for half in range(2):
        top = jnp.concatenate([beside(ms, 4 * u + 2 * half, 2) for u in range(4)], axis=0)
        value = jnp.dot(low, top, preferred_element_type=F32)
        if half:
            right = jnp.concatenate([cross, lower], axis=0)
            value += jnp.dot(high, right, preferred_element_type=F32)
        else:
            value += jnp.dot(high[:, 0:256], upper, preferred_element_type=F32)
            value += lax.dot_general(high[:, 256:512], cross, NT, preferred_element_type=F32)
        finish(middle, 0, part, 4, half, value)

    for i in range(8):
        for e in range(8):
            block = lane_half(middle, e // 2, pl.ds(64 * i, 64), e % 2)
            c = jnp.where(layer == 0, 8, 24) + e
            place_block(meta, counts, i, c, block, stage.at[8 * i + e], out_ref, sem)

    for half, value in product(others, 4, corner):
        finish(y, 0, part, 8, half, value)
    for core in range(2):
        pl.when(layer == core)(
            lambda core=core: emit_edge(core, True, meta, counts, y, stage, 64, out_ref, sem)
        )
    for half in range(2):
        right = jnp.concatenate([beside(ms, 4 * u, 4) for u in (2 * half, 2 * half + 1)], axis=0)
        value = lax.dot_general(high, right, NT, preferred_element_type=F32)
        finish(first_ref, 0, part, 0, half, value)
    pltpu.make_async_copy(stage, stage, sem).wait()


def last_kernel(meta, counts, head, first, mm, _, out_ref, y, stage, sem):
    layer = lax.axis_index("layer")
    for half, value in product(head, 0, mm):
        finish(y, 0, first, 0, half, value)
    for core in range(2):
        pl.when(layer == core)(
            lambda core=core: emit_edge(core, False, meta, counts, y, stage, 0, out_ref, sem)
        )
    pltpu.make_async_copy(stage, stage, sem).wait()


def closing(kernel, meta, counts, inputs, square, blocks, extra, buffers, limit):
    scratch = [pltpu.VMEM((4, 512, 128), BF)] * buffers
    return pl.pallas_call(
        kernel,
        grid_spec=pltpu.PrefetchScalarGridSpec(
            num_scalar_prefetch=2,
            grid=(1,),
            in_specs=[whole(*x.shape) for x in inputs] + [IN_HBM],
            out_specs=[whole(*x.shape) for x in extra] + [IN_HBM],
            scratch_shapes=scratch + [pltpu.VMEM((blocks, 64, 64), BF), pltpu.SemaphoreType.DMA],
        ),
        out_shape=[*extra, jax.ShapeDtypeStruct(square.shape, BF)],
        input_output_aliases={2 + len(inputs): len(extra)},
        compiler_params=pltpu.CompilerParams(vmem_limit_bytes=limit << 20),
        cost_estimate=pl.CostEstimate(
            flops=len(inputs) << 27, bytes_accessed=6 << 20, transcendentals=0
        ),
    )(meta, counts, *inputs, square)


def totals_kernel(scale, sent, _, populations_ref, traces_ref):
    total = jnp.sum(sent[...], axis=0)[:, 0:64]
    populations_ref[...] = total[0:DOM_DEV]
    for n in range(2):
        traces_ref[n] = jnp.sum(total[DOM_DEV + n : DOM_DEV + n + 1]) * scale


def totals(gathered, after, scale):
    return pl.pallas_call(
        functools.partial(totals_kernel, scale),
        in_specs=[pl.BlockSpec(memory_space=pltpu.VMEM), IN_HBM],
        out_specs=[
            pl.BlockSpec(memory_space=pltpu.VMEM),
            pl.BlockSpec(memory_space=pltpu.SMEM),
        ],
        out_shape=[
            jax.ShapeDtypeStruct((DOM_DEV, 64), F32),
            jax.ShapeDtypeStruct((2,), F32),
        ],
        compiler_params=pltpu.CompilerParams(vmem_limit_bytes=16 << 20),
        name="totals",
    )(gathered, after)


def in_hbm(value):
    return pltpu.with_memory_space_constraint(value, pltpu.HBM)


def per_device(density, col_index, counts, domain):
    per_dev, capacity, width = density.shape[:3]
    block_rows = col_index.shape[0]
    radius = (capacity - 1) // 2
    slabs = lax.axis_size("rows")
    devices = slabs * lax.axis_size("layer")
    start = lax.axis_index("rows") * per_dev

    columns = lax.dynamic_slice_in_dim(col_index.T, start, per_dev, 1)
    row_ids = start + jnp.arange(per_dev, dtype=jnp.int32)
    offset = (columns - row_ids[None, :] + radius) % block_rows
    lane = jnp.arange(40, dtype=jnp.int32)
    slots = jnp.arange(capacity, dtype=jnp.int32)
    meta = jnp.sum(
        jnp.where(offset.T[:, :, None] == lane[None, None, :], slots[None, :, None], 0), axis=1
    )

    def device(row, core):
        return (row % slabs) * 2 + core

    ahead = [(device(r, 0), device(r + 1, 0)) for r in range(slabs)]
    ahead += [(device(r, 1), device(r - 1, 1)) for r in range(slabs)]
    across = [(device(r, c), device(r, 1 - c)) for r in range(slabs) for c in range(2)]

    density = in_hbm(density)
    (ss,) = pack(((SYM, 1, 1),), meta, density)
    tiles = ((FULL, 0, 1), (SYM, 0, 0))
    ms, mm, partial = rest(tiles, meta, domain, density, ss, devices)
    ss = lax.ppermute(ss, AXES, ahead)
    ms = lax.ppermute(ms, AXES, ahead)
    mm = lax.ppermute(mm, AXES, ahead)
    gathered = lax.all_to_all(partial, AXES, 0, 0, tiled=True)
    head, others, part, square = local(meta, counts, density, partial)
    corner = lax.ppermute(ss, AXES, across)
    inputs = (head, others, part, ss, ms, corner)
    extra = (jax.ShapeDtypeStruct(head.shape, F32),)
    first, square = closing(middle_kernel, meta, counts, inputs, in_hbm(square), 100, extra, 2, 24)
    inputs = (head, first, mm)
    (square,) = closing(last_kernel, meta, counts, inputs, in_hbm(square), 36, (), 1, 16)
    populations, traces = totals(gathered, in_hbm(square), 1.0 / (block_rows * width))
    return (square, populations, traces)


def solution(mesh):
    placed = (P("rows", None, None, None), P(), P(), P())
    return jax.shard_map(
        per_device,
        mesh=mesh,
        in_specs=placed,
        out_specs=(P(("rows", "layer"), None, None, None), P(("rows", "layer"), None), P()),
        check_vma=False,
    )
```

```python
import functools

import jax
import jax.numpy as jnp
from jax import lax
from jax.experimental import pallas as pl
from jax.experimental.pallas import tpu as pltpu
from jax.sharding import PartitionSpec as P


DOM_DEV = 2
AXES = ("rows", "layer")


def tile_blocks(u, t):
    return [(2 * u + r, 2 * t + s) for r in range(2) for s in range(2)]


OFF = [(u, t) for u in range(4) for t in range(u + 1, 4)]
DIAGONAL = [
    [(0, 0), (0, 1), (2, 2), (2, 3)],
    [(4, 4), (4, 5), (6, 6), (6, 7)],
    [(1, 1), (3, 3), (5, 5), (7, 7)],
]
SYM = [tile_blocks(u, t) for u, t in OFF] + DIAGONAL
FULL = [tile_blocks(u, t) for u in range(4) for t in range(4)]
NT = (((1,), (1,)), ((), ()))
BF = jnp.bfloat16
F32 = jnp.float32
EVERY = pl.ds(0, 512)
IN_HBM = pl.BlockSpec(memory_space=pltpu.HBM)


def issue(groups, meta, density, buf, sems):
    layer = lax.axis_index("layer")
    starts = (8 * layer, 8 * (1 - layer))
    base = 0
    for g, (tiles, near, far) in enumerate(groups):
        row, col = starts[near], starts[far]
        for n, blocks in enumerate(tiles):
            for x, (i, j) in enumerate(blocks):
                slot = meta[row + i, (col - row) + j - i + 16]
                source = density.at[row + i, slot]
                pltpu.make_async_copy(source, buf.at[base + 4 * n + x], sems.at[g]).start()
        base += 4 * len(tiles)


def collect(groups, outs, buf, sems):
    base = 0
    for g, (tiles, _, _) in enumerate(groups):
        span = buf.at[pl.ds(base, 4 * len(tiles))]
        pltpu.make_async_copy(span, span, sems.at[g]).wait()
        for n in range(len(tiles)):
            for r in range(2):
                at = base + 4 * n + 2 * r
                outs[g][n, 64 * r : 64 * r + 64, :] = jnp.concatenate(
                    [buf[at], buf[at + 1]], axis=1
                )
        base += 4 * len(tiles)


def pack_kernel(groups, meta, density, *rest):
    outs, buf, sems = rest[: len(groups)], rest[-2], rest[-1]
    issue(groups, meta, density, buf, sems)
    collect(groups, outs, buf, sems)


def pack(groups, meta, density):
    sizes = [len(tiles) for tiles, _, _ in groups]
    return pl.pallas_call(
        functools.partial(pack_kernel, groups),
        grid_spec=pltpu.PrefetchScalarGridSpec(
            num_scalar_prefetch=1,
            grid=(1,),
            in_specs=[IN_HBM],
            out_specs=[pl.BlockSpec((n, 128, 128), lambda i, m: (0, 0, 0)) for n in sizes],
            scratch_shapes=[
                pltpu.VMEM((4 * sum(sizes), 64, 64), BF),
                pltpu.SemaphoreType.DMA((len(sizes),)),
            ],
        ),
        out_shape=[jax.ShapeDtypeStruct((n, 128, 128), BF) for n in sizes],
        compiler_params=pltpu.CompilerParams(vmem_limit_bytes=16 << 20),
        cost_estimate=pl.CostEstimate(
            flops=0, bytes_accessed=sum(sizes) << 17, transcendentals=0
        ),
        name="pack",
    )(meta, density)


def rest_kernel(groups, meta, domain, density, _, *rest):
    outs, out_ref = rest[: len(groups)], rest[len(groups)]
    buf, packed, rows_ref, sems, sums = rest[len(groups) + 1 :]
    layer = lax.axis_index("layer")
    start = 16 * lax.axis_index("rows")
    base = 8 * layer
    issue(groups, meta, density, buf, packed)
    for i in range(4):
        source = density.at[pl.ds(base + 2 * i, 2)]
        pltpu.make_async_copy(source, rows_ref.at[pl.ds(2 * i, 2)], sems.at[i]).start()
    out_ref[...] = jnp.zeros_like(out_ref)
    sums[...] = jnp.zeros_like(sums)
    eye = lax.broadcasted_iota(jnp.int32, (64, 64), 0) == lax.broadcasted_iota(
        jnp.int32, (64, 64), 1
    )
    sub = lax.broadcasted_iota(jnp.int32, (8, 64), 0)
    collect(groups, outs, buf, packed)

    @pl.loop(0, 4)
    def _(u):
        pltpu.make_async_copy(
            density.at[pl.ds(0, 2)], rows_ref.at[pl.ds(2 * u, 2)], sems.at[u]
        ).wait()
        for r in range(2):
            i = 2 * u + r
            k = base + i
            total = jnp.zeros((64, 64), F32)
            for s in range(rows_ref.shape[1]):
                block = rows_ref[i, s].astype(F32)
                total += block * block
            column = jnp.sum(total, axis=1, keepdims=True)
            squares = jnp.sum(jnp.where(eye, column, 0.0), axis=0, keepdims=True)
            squares = squares.astype(BF).astype(F32)
            middle = rows_ref[i, meta[k, 16]].astype(F32)
            diagonal = jnp.sum(jnp.where(eye, middle, 0.0), axis=0, keepdims=True)
            target = domain[start + k]
            owner = target // DOM_DEV
            place = target - owner * DOM_DEV
            out_ref[owner, :, 0:64] = out_ref[owner, :, 0:64] + jnp.where(
                sub == place, squares, 0.0
            )
            sums[:, 0:64] = sums[:, 0:64] + jnp.where(
                sub == DOM_DEV, diagonal, jnp.where(sub == DOM_DEV + 1, squares, 0.0)
            )

    out_ref[...] = out_ref[...] + sums[...][None]


def rest(groups, meta, domain, density, after, devices):
    capacity = density.shape[1]
    sizes = [len(tiles) for tiles, _, _ in groups]
    shapes = [(n, 128, 128) for n in sizes] + [(devices, 8, 128)]
    return pl.pallas_call(
        functools.partial(rest_kernel, groups),
        grid_spec=pltpu.PrefetchScalarGridSpec(
            num_scalar_prefetch=2,
            grid=(1,),
            in_specs=[IN_HBM, IN_HBM],
            out_specs=[pl.BlockSpec(shape, lambda i, m, d: (0, 0, 0)) for shape in shapes],
            scratch_shapes=[
                pltpu.VMEM((max(4 * sum(sizes), 1), 64, 64), BF),
                pltpu.SemaphoreType.DMA((max(len(sizes), 1),)),
                pltpu.VMEM((8, capacity, 64, 64), BF),
                pltpu.SemaphoreType.DMA((4,)),
                pltpu.VMEM((8, 128), F32),
            ],
        ),
        out_shape=[
            jax.ShapeDtypeStruct(shape, F32 if n == len(sizes) else BF)
            for n, shape in enumerate(shapes)
        ],
        compiler_params=pltpu.CompilerParams(vmem_limit_bytes=16 << 20),
        cost_estimate=pl.CostEstimate(flops=0, bytes_accessed=8 << 20, transcendentals=0),
        name="rest",
    )(meta, domain, density, after)


def spread(slots, block, own, first, at, k):
    zero = jnp.zeros((64, 64), BF)
    for r in range(2):
        rows = pl.ds(pl.multiple_of(at + 64 * r, 64), 64)
        for pp in range(17):
            halves = []
            for s in range(2):
                d = 2 * pp + s - r
                halves.append(block(r, slots[k + r, d]) if 0 <= d <= 32 else zero)
            own[first + pp, rows, :] = jnp.concatenate(halves, axis=1)


def octant(layer, q):
    return jnp.where(layer == 0, q, 5 - q)


def wide(ref, pair, rows):
    return jnp.concatenate([ref[pair, rows, :], ref[pair + 1, rows, :]], axis=1)


def local_kernel(meta, counts, density, _, head_ref, rest_ref, part_ref, out_ref, *scratch):
    rows_ref, sems, mine, other, near_ref, stage, sent = scratch
    layer = lax.axis_index("layer")
    base = 8 * layer
    sib = 8 * (1 - layer)
    for n in range(8):
        source = density.at[pl.ds((base if n < 4 else sib) + 2 * (n % 4), 2)]
        pltpu.make_async_copy(source, rows_ref.at[pl.ds(2 * n, 2)], sems.at[n]).start()

    @pl.loop(0, 24)
    def _(p):
        mine[p] = jnp.zeros(mine.shape[1:], BF)
        other[p] = jnp.zeros(other.shape[1:], BF)

    def gather(u, own, first, at, k):
        pltpu.make_async_copy(
            density.at[pl.ds(0, 2)], rows_ref.at[pl.ds(2 * u, 2)], sems.at[u]
        ).wait()
        spread(meta, lambda r, slot: rows_ref[2 * u + r, slot], own, first, at, k)

    @pl.loop(0, 4)
    def _(u):
        gather(u, mine, 4 * layer + u, 128 * u, base + 2 * u)

    at = [4 * octant(layer, q) for q in range(5)]
    every = pl.ds(0, 512)

    def put(ref, base, half, value):
        ref[base + 2 * half] = value[:, 0:128].astype(ref.dtype)
        ref[base + 2 * half + 1] = value[:, 128:256].astype(ref.dtype)

    def left(ref, octs, rows):
        return jnp.concatenate(
            [wide(ref, at[q] + 2 * h, rows) for q in octs for h in range(2)], axis=1
        )

    def own(base, octs, source):
        for half in range(2):
            right = left(source, octs, pl.ds(256 * half, 256))
            value = lax.dot_general(left(mine, octs, every), right, NT, preferred_element_type=F32)
            put(near_ref, base, half, value)

    def toward(ref, base, q, octs):
        for half in range(2):
            right = jnp.concatenate(
                [wide((mine, other)[o - 2], at[q] + 2 * half, every) for o in octs], axis=0
            )
            value = jnp.dot(left(mine, octs, every), right, preferred_element_type=F32)
            put(ref, base, half, value)

    for p in range(4):
        head_ref[p] = mine[at[0] + p]
        rest_ref[p] = mine[at[1] + p]
        rest_ref[4 + p] = mine[at[4] + p]

    def emit(base, first):
        for i in range(8):
            for e in range(8):
                n = 8 * base + 8 * i + e
                block = lane_half(near_ref, base // 2 + e // 2, pl.ds(64 * i, 64), e % 2)
                place_block(meta, counts, i, first + e, block, stage.at[n], out_ref, sent)

    own(0, (0, 1, 2, 3, 4), mine)
    emit(0, 16)
    toward(part_ref, 0, 0, (2,))

    @pl.loop(0, 4)
    def _(u):
        gather(u + 4, other, 4 * (1 - layer) + u, 128 * u, sib + 2 * u)

    own(4, (1, 2, 3, 4), other)
    emit(8, jnp.where(layer == 0, 24, 8))
    toward(part_ref, 4, 1, (2, 3))
    toward(part_ref, 8, 4, (2, 3))
    pltpu.make_async_copy(stage, stage, sent).wait()


def whole(*shape):
    return pl.BlockSpec(shape, lambda i, m, c: (0, 0, 0))


def local(meta, counts, density, after):
    capacity = density.shape[1]
    parts = ((4, BF), (8, BF), (12, F32))
    return pl.pallas_call(
        local_kernel,
        grid_spec=pltpu.PrefetchScalarGridSpec(
            num_scalar_prefetch=2,
            grid=(1,),
            in_specs=[IN_HBM, IN_HBM],
            out_specs=[whole(n, 512, 128) for n, _ in parts] + [IN_HBM],
            scratch_shapes=[
                pltpu.VMEM((16, capacity, 64, 64), BF),
                pltpu.SemaphoreType.DMA((8,)),
                pltpu.VMEM((24, 512, 128), BF),
                pltpu.VMEM((24, 512, 128), BF),
                pltpu.VMEM((8, 512, 128), BF),
                pltpu.VMEM((128, 64, 64), BF),
                pltpu.SemaphoreType.DMA,
            ],
        ),
        out_shape=[jax.ShapeDtypeStruct((n, 512, 128), t) for n, t in parts]
        + [jax.ShapeDtypeStruct((8, capacity, 64, 64), BF)],
        compiler_params=pltpu.CompilerParams(vmem_limit_bytes=36 << 20),
        cost_estimate=pl.CostEstimate(
            flops=4 << 30, bytes_accessed=16 << 20, transcendentals=0
        ),
        name="local",
    )(meta, counts, density, after)


def beside(tiles, base, count):
    return jnp.concatenate([tiles[base + n] for n in range(count)], axis=1)


def corners(tiles_ref):
    tile = {ut: tiles_ref[n] for n, ut in enumerate(OFF)}
    for u in range(4):
        top = tiles_ref[6 + u // 2, 64 * (u % 2) : 64 * (u % 2) + 64, :]
        below = tiles_ref[8, 64 * (u // 2) : 64 * (u // 2) + 64, :]
        below = below[:, 64 * (u % 2) : 64 * (u % 2) + 64]
        bottom = jnp.concatenate([top[:, 64:128].T, below], axis=1)
        tile[u, u] = jnp.concatenate([top, bottom], axis=0)

    def square(u):
        top = jnp.concatenate([tile[u, u], tile[u, u + 1]], axis=1)
        bottom = jnp.concatenate([tile[u, u + 1].T, tile[u + 1, u + 1]], axis=1)
        return jnp.concatenate([top, bottom], axis=0)

    cross = jnp.concatenate(
        [jnp.concatenate([tile[u, 2], tile[u, 3]], axis=1) for u in range(2)], axis=0
    )
    return square(0), cross, square(2)


def product(ref, base, tiles_ref):
    upper, cross, lower = corners(tiles_ref)
    low, high = wide(ref, base, EVERY), wide(ref, base + 2, EVERY)
    yield 0, jnp.dot(low, upper, preferred_element_type=F32) + lax.dot_general(
        high, cross, NT, preferred_element_type=F32
    )
    yield 1, jnp.dot(
        jnp.concatenate([low, high], axis=1),
        jnp.concatenate([cross, lower], axis=0),
        preferred_element_type=F32,
    )


def lane_half(ref, pair, rows, odd):
    return ref[pair, rows, :][:, 64 * odd : 64 * odd + 64]


def place_block(meta, counts, i, c, block, stage, out_ref, sem):
    k = 8 * lax.axis_index("layer") + i
    slot = meta[k, c - i]
    live = slot < counts[16 * lax.axis_index("rows") + k]
    stage[...] = jnp.where(live, block, jnp.zeros_like(block))
    pltpu.make_async_copy(stage, out_ref.at[i, slot], sem).start()


def finish(ref, at, partial, base, half, value):
    for s in range(2):
        p = 2 * half + s
        total = partial[base + p] + value[:, 128 * s : 128 * s + 128]
        ref[at + p] = total.astype(ref.dtype)


def emit_edge(core, near, meta, counts, ref, stage, at, out_ref, sem):
    above = near == (core == 1)
    n = at
    for i in range(8):
        for e in range(i, 8) if above else range(i + 1):
            block = lane_half(ref, e // 2, pl.ds(64 * i, 64), e % 2)
            c = e if above else 32 + e
            place_block(meta, counts, i, c, block, stage.at[n], out_ref, sem)
            n += 1


def middle_kernel(
    meta, counts, head, others, part, ss, ms, corner, _, first_ref, out_ref, y, middle, stage, sem
):
    layer = lax.axis_index("layer")
    upper, cross, lower = corners(ss)
    high = jnp.concatenate([wide(others, 0, EVERY), wide(others, 2, EVERY)], axis=1)
    low = jnp.concatenate([wide(head, 0, EVERY), wide(head, 2, EVERY)], axis=1)
    for half in range(2):
        top = jnp.concatenate([beside(ms, 4 * u + 2 * half, 2) for u in range(4)], axis=0)
        value = jnp.dot(low, top, preferred_element_type=F32)
        if half:
            right = jnp.concatenate([cross, lower], axis=0)
            value += jnp.dot(high, right, preferred_element_type=F32)
        else:
            value += jnp.dot(high[:, 0:256], upper, preferred_element_type=F32)
            value += lax.dot_general(high[:, 256:512], cross, NT, preferred_element_type=F32)
        finish(middle, 0, part, 4, half, value)

    for i in range(8):
        for e in range(8):
            block = lane_half(middle, e // 2, pl.ds(64 * i, 64), e % 2)
            c = jnp.where(layer == 0, 8, 24) + e
            place_block(meta, counts, i, c, block, stage.at[8 * i + e], out_ref, sem)

    for half, value in product(others, 4, corner):
        finish(y, 0, part, 8, half, value)
    for core in range(2):
        pl.when(layer == core)(
            lambda core=core: emit_edge(core, True, meta, counts, y, stage, 64, out_ref, sem)
        )
    for half in range(2):
        right = jnp.concatenate([beside(ms, 4 * u, 4) for u in (2 * half, 2 * half + 1)], axis=0)
        value = lax.dot_general(high, right, NT, preferred_element_type=F32)
        finish(first_ref, 0, part, 0, half, value)
    pltpu.make_async_copy(stage, stage, sem).wait()


def last_kernel(meta, counts, head, first, mm, _, out_ref, y, stage, sem):
    layer = lax.axis_index("layer")
    for half, value in product(head, 0, mm):
        finish(y, 0, first, 0, half, value)
    for core in range(2):
        pl.when(layer == core)(
            lambda core=core: emit_edge(core, False, meta, counts, y, stage, 0, out_ref, sem)
        )
    pltpu.make_async_copy(stage, stage, sem).wait()


def closing(kernel, meta, counts, inputs, square, blocks, extra, buffers, limit):
    scratch = [pltpu.VMEM((4, 512, 128), BF)] * buffers
    return pl.pallas_call(
        kernel,
        grid_spec=pltpu.PrefetchScalarGridSpec(
            num_scalar_prefetch=2,
            grid=(1,),
            in_specs=[whole(*x.shape) for x in inputs] + [IN_HBM],
            out_specs=[whole(*x.shape) for x in extra] + [IN_HBM],
            scratch_shapes=scratch + [pltpu.VMEM((blocks, 64, 64), BF), pltpu.SemaphoreType.DMA],
        ),
        out_shape=[*extra, jax.ShapeDtypeStruct(square.shape, BF)],
        input_output_aliases={2 + len(inputs): len(extra)},
        compiler_params=pltpu.CompilerParams(vmem_limit_bytes=limit << 20),
        cost_estimate=pl.CostEstimate(
            flops=len(inputs) << 27, bytes_accessed=6 << 20, transcendentals=0
        ),
    )(meta, counts, *inputs, square)


def totals_kernel(scale, sent, _, populations_ref, traces_ref):
    total = jnp.sum(sent[...], axis=0)[:, 0:64]
    populations_ref[...] = total[0:DOM_DEV]
    for n in range(2):
        traces_ref[n] = jnp.sum(total[DOM_DEV + n : DOM_DEV + n + 1]) * scale


def totals(gathered, after, scale):
    return pl.pallas_call(
        functools.partial(totals_kernel, scale),
        in_specs=[pl.BlockSpec(memory_space=pltpu.VMEM), IN_HBM],
        out_specs=[
            pl.BlockSpec(memory_space=pltpu.VMEM),
            pl.BlockSpec(memory_space=pltpu.SMEM),
        ],
        out_shape=[
            jax.ShapeDtypeStruct((DOM_DEV, 64), F32),
            jax.ShapeDtypeStruct((2,), F32),
        ],
        compiler_params=pltpu.CompilerParams(vmem_limit_bytes=16 << 20),
        name="totals",
    )(gathered, after)


def in_hbm(value):
    return pltpu.with_memory_space_constraint(value, pltpu.HBM)


def per_device(density, col_index, counts, domain):
    per_dev, capacity, width = density.shape[:3]
    block_rows = col_index.shape[0]
    radius = (capacity - 1) // 2
    slabs = lax.axis_size("rows")
    devices = slabs * lax.axis_size("layer")
    start = lax.axis_index("rows") * per_dev

    columns = lax.dynamic_slice_in_dim(col_index.T, start, per_dev, 1)
    row_ids = start + jnp.arange(per_dev, dtype=jnp.int32)
    offset = (columns - row_ids[None, :] + radius) % block_rows
    lane = jnp.arange(40, dtype=jnp.int32)
    slots = jnp.arange(capacity, dtype=jnp.int32)
    meta = jnp.sum(
        jnp.where(offset.T[:, :, None] == lane[None, None, :], slots[None, :, None], 0), axis=1
    )

    def device(row, core):
        return (row % slabs) * 2 + core

    ahead = [(device(r, 0), device(r + 1, 0)) for r in range(slabs)]
    ahead += [(device(r, 1), device(r - 1, 1)) for r in range(slabs)]
    across = [(device(r, c), device(r, 1 - c)) for r in range(slabs) for c in range(2)]

    density = in_hbm(density)
    (ss,) = pack(((SYM, 1, 1),), meta, density)
    tiles = ((FULL, 0, 1), (SYM, 0, 0))
    ms, mm = pack(tiles, meta, density)
    (partial,) = rest((), meta, domain, density, mm, devices)
    ss = lax.ppermute(ss, AXES, ahead)
    ms = lax.ppermute(ms, AXES, ahead)
    mm = lax.ppermute(mm, AXES, ahead)
    gathered = lax.all_to_all(partial, AXES, 0, 0, tiled=True)
    head, others, part, square = local(meta, counts, density, partial)
    corner = lax.ppermute(ss, AXES, across)
    inputs = (head, others, part, ss, ms, corner)
    extra = (jax.ShapeDtypeStruct(head.shape, F32),)
    first, square = closing(middle_kernel, meta, counts, inputs, in_hbm(square), 100, extra, 2, 24)
    inputs = (head, first, mm)
    (square,) = closing(last_kernel, meta, counts, inputs, in_hbm(square), 36, (), 1, 16)
    populations, traces = totals(gathered, in_hbm(square), 1.0 / (block_rows * width))
    return (square, populations, traces)


def solution(mesh):
    placed = (P("rows", None, None, None), P(), P(), P())
    return jax.shard_map(
        per_device,
        mesh=mesh,
        in_specs=placed,
        out_specs=(P(("rows", "layer"), None, None, None), P(("rows", "layer"), None), P()),
        check_vma=False,
    )
```
